32 devices in a mesh: seq: 8 (over z, x), head: 4 (over y, core).
Axes of the slice: x: 2, y: 2, z: 4, core: 2. Of those that a mesh axis runs over, the one named last changes fastest.
Arguments:
- queries: bfloat16 [1024, 1536], P('seq', 'head'), may hold values from -8 to 8
- cell_types: int32 [1024], P('seq'), may hold values from 0 to 127
- promoters: int32 [1024], P('seq'), may hold values from 0 to 16383, as said below
- offsets: int32 [1024], P('seq'), may hold values from -64 to 64, as said below
- cell_embed: bfloat16 [128, 1536], P(None, 'head'), may hold values from -3 to 3
- bin_keys: bfloat16 [16384, 1536], P('seq', 'head'), may hold values from -6 to 6
- bin_values: bfloat16 [16384, 1536], P('seq', 'head'), may hold values from -6 to 6
- slopes: float32 [16], P('head'), may hold values from 1.280082e-05 to 0.05
- w_out: bfloat16 [1536, 1536], P('head'), may hold values from -0.15625 to 0.15625
Outputs:
- pooled_features: bfloat16 [1024, 1536], P('seq', 'head')
The draws below stay inside these ranges and needn't reach their ends.
Inputs may be any that keep to these rules, and one draw needn't show every extreme that they name: `promoters`: the promoter of row r lies in bins (r // 128) * 2048 to (r // 128 + 1) * 2048 - 1; in each aligned block of 128 rows, the block's first row sits at the first of those bins and its second row at the last. `offsets`: in each aligned block of 128 rows the first row has offset -64 and the second row 64.
All inputs are finite; a program needn't handle non-finite values.
Results may differ from the reference program's by a relative error of at most 0.012.
Values may be sent and summed in bfloat16 or wider, within the bound.
A program may use at most 128 MiB of HBM per device.

```python
import math
import jax
import jax.numpy as jnp
from jax import lax

HEADS = 16
HEAD_DIM = 96
D = 1536
CT = 128
BIN_DEV = 2048
Q_DEV = 128
RADIUS = 7812
SHIFT = 64
HOPS = 4
BINS = 16384
Q_ALL = 1024
N_SEQ = 8


def positions(key):
    base = jax.random.fold_in(key, 7101)
    first, second, third = jax.random.split(base, 3)
    index = jnp.arange(Q_ALL, dtype=jnp.int32)
    block = index // Q_DEV
    within = index % Q_DEV
    inner = jnp.minimum(jax.random.randint(first, (Q_ALL,), 0, BIN_DEV), jax.random.randint(second, (Q_ALL,), 0, BIN_DEV))
    inner = jnp.where(within == 0, 0, jnp.where(within == 1, BIN_DEV - 1, inner))
    shifts = jax.random.randint(third, (Q_ALL,), -SHIFT, SHIFT + 1)
    shifts = jnp.where(within == 0, -SHIFT, jnp.where(within == 1, SHIFT, shifts))
    return ((block * BIN_DEV + inner).astype(jnp.int32), shifts.astype(jnp.int32))


def draw_promoters(key, part):
    return positions(key)[0]


def draw_offsets(key, part):
    return positions(key)[1]


def draw_bin_keys(key, part):
    inner_key = jax.random.fold_in(key, 7202)
    table = jnp.clip(jax.random.normal(inner_key, (BINS, D)), -6.0, 6.0)
    return table.astype(jnp.bfloat16)


def draw_queries(key, part):
    inner_key = jax.random.fold_in(key, 7303)
    table = jnp.clip(jax.random.normal(inner_key, (Q_ALL, D)), -6.0, 6.0)
    return table.astype(jnp.bfloat16)


def set_ends(entries, rng, least, largest):
    place = [jax.random.randint(jax.random.fold_in(rng, axis), (), 0, length) for axis, length in enumerate(entries.shape)]
    main_axis = entries.shape.index(max(entries.shape))
    neighbour = place[:main_axis] + [(place[main_axis] + 1) % entries.shape[main_axis]] + place[main_axis + 1:]
    return entries.at[tuple(place)].set(least).at[tuple(neighbour)].set(largest)


def block_scale(stream_key, dims, pieces, least, largest):
    level, own = 1.0, jax.random.fold_in(stream_key, 6)
    for dim, shards_of in pieces:
        steps = jnp.exp(jax.random.uniform(jax.random.fold_in(own, dim), (shards_of,), jnp.float32, least / len(pieces), largest / len(pieces)))
        level = level * jnp.repeat(steps, dims[dim] // shards_of).reshape([-1 if axis == dim else 1 for axis in range(len(dims))])
    return level


def noise(stream_key, extent, spread, reach, cuts=(), kind=jnp.bfloat16):
    loudness = block_scale(stream_key, extent, cuts, -0.22, 0.18) if cuts else 1.0
    entries = jax.random.normal(stream_key, extent, jnp.float32) * spread * loudness
    return jnp.minimum(jnp.maximum(entries, -reach), reach).astype(kind)


def setup_inputs(seed: int = 0) -> dict:
    seeds = jax.random.split(jax.random.key(seed), 10)
    queries = draw_queries(jax.random.fold_in(seeds[9], 71), 0)
    cell_types = set_ends(jax.random.randint(seeds[1], (Q_ALL,), 0, CT), jax.random.fold_in(seeds[1], 1), 0, CT - 1).astype(jnp.int32)
    promoters = draw_promoters(jax.random.fold_in(seeds[9], 71), 0)
    offsets = draw_offsets(jax.random.fold_in(seeds[9], 71), 0)
    cell_embed = noise(seeds[4], (CT, D), 0.5, 3.0, ((1, 4),))
    bin_keys = draw_bin_keys(jax.random.fold_in(seeds[9], 71), 0)
    bin_values = noise(seeds[6], (BINS, D), 1.0, 6.0, ((0, 8), (1, 4)))
    slopes = jnp.clip(jnp.exp(math.log(0.05) - 8.270269 * jax.random.uniform(seeds[7], (HEADS,), jnp.float32) ** block_scale(seeds[7], (HEADS,), ((0, 4),), -0.2, 0.2)), 1.2800819604308344e-05, 0.05)
    w_out = noise(seeds[8], (D, D), D ** -0.5, 0.15625, ((0, 4),))
    return dict(queries=queries, cell_types=cell_types, promoters=promoters, offsets=offsets, cell_embed=cell_embed, bin_keys=bin_keys, bin_values=bin_values, slopes=slopes, w_out=w_out)


def reference(queries, cell_types, promoters, offsets, cell_embed, bin_keys, bin_values, slopes, w_out):
    embedded = cell_embed.astype(jnp.float32)[cell_types]
    query_rows = (queries.astype(jnp.float32) + embedded).astype(jnp.bfloat16)
    centres = promoters + offsets
    padding = HOPS * BIN_DEV
    keys_padded = jnp.pad(bin_keys, ((padding, padding), (0, 0)))
    values_padded = jnp.pad(bin_values, ((padding, padding), (0, 0)))
    window_len = (2 * HOPS + 1) * BIN_DEV
    scale = HEAD_DIM ** -0.5

    def one_shard(shard):
        shard_rows = lax.dynamic_slice_in_dim(query_rows, shard * Q_DEV, Q_DEV, 0)
        shard_centres = lax.dynamic_slice_in_dim(centres, shard * Q_DEV, Q_DEV, 0)
        shard_keys = lax.dynamic_slice_in_dim(keys_padded, shard * BIN_DEV, window_len, 0)
        shard_values = lax.dynamic_slice_in_dim(values_padded, shard * BIN_DEV, window_len, 0)
        bin_index = (shard - HOPS) * BIN_DEV + jnp.arange(window_len, dtype=jnp.int32)
        distance = jnp.abs(bin_index[None, :] - shard_centres[:, None])
        usable = (distance <= RADIUS) & (bin_index[None, :] >= 0) & (bin_index[None, :] < BINS)
        distance_float = distance.astype(jnp.float32)
        head_queries = shard_rows.reshape(Q_DEV, HEADS, HEAD_DIM).transpose(1, 0, 2)
        head_keys = shard_keys.reshape(window_len, HEADS, HEAD_DIM).transpose(1, 0, 2)
        head_values = shard_values.reshape(window_len, HEADS, HEAD_DIM).transpose(1, 0, 2)

        def one_head(inputs):
            query_head, key_head, value_head, slope = inputs
            scores = jnp.dot(query_head, key_head.T, preferred_element_type=jnp.float32) * scale
            scores = scores - slope * distance_float
            scores = jnp.where(usable, scores, -1e30)
            row_max = jnp.max(scores, axis=1, keepdims=True)
            exps = jnp.where(usable, jnp.exp(scores - row_max), 0.0)
            totals = jnp.sum(exps, axis=1)
            weights = exps.astype(jnp.bfloat16)
            pooled_head = jnp.dot(weights, value_head, preferred_element_type=jnp.float32)
            return pooled_head / totals[:, None]

        pooled_heads = lax.map(one_head, (head_queries, head_keys, head_values, slopes))
        return pooled_heads.transpose(1, 0, 2).reshape(Q_DEV, D).astype(jnp.bfloat16)

    pooled = lax.map(one_shard, jnp.arange(N_SEQ, dtype=jnp.int32)).reshape(Q_ALL, D)
    return jnp.dot(pooled, w_out, preferred_element_type=jnp.float32).astype(jnp.bfloat16)
```

```python
import functools

import jax
import jax.numpy as jnp
from jax import lax
from jax.experimental import pallas as pl
from jax.experimental.pallas import tpu as pltpu
from jax.sharding import PartitionSpec as P

HEAD_DIM = 96
RADIUS = 7812
SHIFT = 64
HOPS = 4
LANES = 128
CHUNK = 256
EXTRA = 16
LOG2E = 1.4426950408889634
FAR = -1e30


MESH = pl.DeviceIdType.MESH


def placed(head):
    tile, offset = divmod(head * HEAD_DIM, LANES)
    return tile, offset, (offset + HEAD_DIM) % LANES


def spare_lanes(shape, free):
    lane = lax.broadcasted_iota(jnp.int32, shape, len(shape) - 1) - free
    return lane, (lane >= 0) & (lane < LANES - HEAD_DIM)


def head_tile(rows_ref, head):
    tile, offset, _ = placed(head)
    own = rows_ref[:, tile * LANES : (tile + 1) * LANES]
    if offset + HEAD_DIM > LANES:
        other = rows_ref[:, (tile + 1) * LANES : (tile + 2) * LANES]
        lane = lax.broadcasted_iota(jnp.int32, own.shape, 1)
        own = jnp.where(lane >= offset, own, other)
    return own


def prepare_keys(k_ref, keys_ref):
    for begin in range(0, k_ref.shape[0], CHUNK):
        index = lax.broadcasted_iota(jnp.int32, (CHUNK, LANES), 0) + begin
        for head in range(keys_ref.shape[0]):
            _, _, free = placed(head)
            lane, inner = spare_lanes((CHUNK, LANES), free)
            part = jnp.where(lane % 2 == 0, index // 256, index % 256)
            part = part.astype(jnp.float32).astype(jnp.bfloat16)
            tile = head_tile(k_ref.at[begin : begin + CHUNK], head)
            keys_ref[head, begin : begin + CHUNK, :] = jnp.where(inner, part, tile)


def prepare_values(v_ref, values_ref):
    for begin in range(0, v_ref.shape[0], CHUNK):
        turned = v_ref[begin : begin + CHUNK, :].astype(jnp.float32).T.astype(jnp.bfloat16)
        values_ref[:, begin : begin + CHUNK] = turned


def prepare_query(rows_ref, head, slope, sign):
    _, _, free = placed(head)
    scaled = head_tile(rows_ref, head).astype(jnp.float32) * (LOG2E * HEAD_DIM**-0.5)
    high = scaled.astype(jnp.bfloat16)
    low = (scaled - high.astype(jnp.float32)).astype(jnp.bfloat16)
    bias = jnp.full((1, LANES), slope * -sign, jnp.float32)
    first = bias.astype(jnp.bfloat16).astype(jnp.float32)
    second = (bias - first).astype(jnp.bfloat16).astype(jnp.float32)
    third = (bias - first - second).astype(jnp.bfloat16).astype(jnp.float32)
    lane, _ = spare_lanes((1, LANES), free)
    weight = jnp.where(lane % 2 == 0, 256.0, 1.0)
    near, far = (lane >= 0) & (lane < 2), (lane >= 2) & (lane < 4)
    upper = jnp.where(near, first, jnp.where(far, second, 0.0)) * weight
    lower = jnp.where(near, third, 0.0) * weight
    _, inner = spare_lanes(scaled.shape, free)
    high = jnp.where(inner, upper.astype(jnp.bfloat16), high)
    low = jnp.where(inner, lower.astype(jnp.bfloat16), low)
    return jnp.concatenate([high, low], axis=1)


def attend(columns, slots, pack_ref, keys_ref, values_ref, slope_ref, score_ref, out_ref, stat_ref):
    groups, bins, _ = keys_ref.shape
    rows = pack_ref.shape[1] - EXTRA
    within = []
    for slot in slots:
        corner = pack_ref[slot, rows:, :rows].astype(jnp.float32)
        within.append(corner[0:1] * 256.0 + corner[1:2])
    aheads = [hop * bins - sign * inside for (hop, sign), inside in zip(columns, within)]
    first, last = bins, 0
    for begin in range(0, bins, CHUNK):
        for hop, sign in columns:
            nearest = hop * bins + (begin - bins + 1 if sign > 0 else 1 - begin - CHUNK) - SHIFT
            if hop < 2 or nearest <= RADIUS:
                first, last = min(first, begin), max(last, begin + CHUNK)
    sublane = lax.broadcasted_iota(jnp.int32, (8, rows), 0).astype(jnp.float32)

    def biased(column, start, slope, score):
        hop, sign = columns[column]
        index = sublane + float(start)
        if hop == 0 or (hop == 1 and (start < SHIFT if sign > 0 else start + 8 > bins - SHIFT)):
            before = jnp.maximum(-(index * sign + aheads[column]), 0.0)
            score = score - (2.0 * slope) * before
        farthest = hop * bins + (start + 7 if sign > 0 else bins - 1 - start) + SHIFT
        if farthest > RADIUS:
            score = jnp.where(index * sign <= RADIUS - aheads[column], score, FAR)
        return score

    def scores(head):
        slope = slope_ref[head] * LOG2E
        query = [
            prepare_query(pack_ref.at[slot, :rows], head, slope, float(sign))
            for slot, (hop, sign) in zip(slots, columns)
        ]
        query = jnp.concatenate(query, axis=0) if len(slots) > 1 else query[0]
        tops = [None] * len(slots)
        for begin in range(first, last, CHUNK):
            keys = keys_ref[head, begin : begin + CHUNK, :]
            raw = lax.dot_general(
                jnp.concatenate([keys, keys], axis=1),
                query,
                (((1,), (1,)), ((), ())),
                preferred_element_type=jnp.float32,
            )
            for start in range(0, CHUNK, 8):
                for i in range(len(slots)):
                    lanes = slice(i * rows, (i + 1) * rows)
                    score = biased(i, begin + start, slope, raw[start : start + 8, lanes])
                    score_ref[head % 2, begin + start : begin + start + 8, lanes] = score
                    tops[i] = score if tops[i] is None else jnp.maximum(tops[i], score)
        return [jnp.maximum(jnp.max(top, axis=0, keepdims=True), 0.1 * FAR) for top in tops]

    def pool(head, peaks):
        totals = [None] * len(slots)
        weights = []
        for begin in range(first, last, CHUNK):
            parts = []
            for i in range(len(slots)):
                lanes = slice(i * rows, (i + 1) * rows)
                exps = jnp.exp2(score_ref[head % 2, begin : begin + CHUNK, lanes] - peaks[i])
                total = jnp.sum(exps.reshape(CHUNK // 8, 8, rows), axis=0)
                totals[i] = total if totals[i] is None else totals[i] + total
                parts.append(exps.astype(jnp.bfloat16))
            weights.append(jnp.concatenate(parts, axis=1) if len(slots) > 1 else parts[0])
        gained = jnp.dot(
            values_ref[head * HEAD_DIM : (head + 1) * HEAD_DIM, first:last],
            jnp.concatenate(weights, axis=0),
            preferred_element_type=jnp.float32,
        )
        slope = slope_ref[head] * LOG2E
        for i, slot in enumerate(slots):
            out_ref[slot, head * HEAD_DIM : (head + 1) * HEAD_DIM, :] = gained[
                :, i * rows : (i + 1) * rows
            ].astype(jnp.bfloat16)
            stat_ref[slot, head : head + 1, :] = peaks[i] - slope * aheads[i]
            stat_ref[slot, groups + head : groups + head + 1, :] = jnp.sum(
                totals[i], axis=0, keepdims=True
            )

    peaks = scores(0)
    for head in range(groups):
        later = scores(head + 1) if head + 1 < groups else None
        pool(head, peaks)
        peaks = later


def attend_kernel(
    hops, seq_count, head_count,
    query_ref, type_ref, promoter_ref, offset_ref, embed_ref, k_hbm, v_hbm, w_hbm, slope_ref,
    result_ref,
    k_ref, v_ref, keys_ref, values_ref, w_ref, pack_ref, out_ref, stat_ref, back_ref, back_stat_ref,
    score_ref, sum_ref, part_ref, head_ref,
    load_sem, q_send, q_recv, o_send, o_recv, s_send, s_recv, h_send, h_recv,
):
    position = lax.axis_index("seq")
    mine = lax.axis_index("head")
    width, rows = out_ref.shape[1:]
    groups = width // HEAD_DIM
    piece = result_ref.shape[1]
    loads = [
        pltpu.make_async_copy(src, dst, load_sem.at[i])
        for i, (src, dst) in enumerate(((k_hbm, k_ref), (v_hbm, v_ref), (w_hbm, w_ref)))
    ]
    for load in loads:
        load.start()

    def inside(index):
        return (index >= 0) & (index < seq_count)

    barrier = pltpu.get_barrier_semaphore()
    offsets = [sign * hop for hop in range(1, hops + 1) for sign in (1, -1)]
    for d in offsets:

        @pl.when(inside(position + d))
        def _(d=d):
            pl.semaphore_signal(
                barrier, inc=1, device_id=(position + d, mine), device_id_type=MESH
            )

    for r in range(1, head_count):
        pl.semaphore_signal(
            barrier, inc=1, device_id=(position, lax.rem(mine + r, head_count)), device_id_type=MESH
        )

    bins = k_ref.shape[0]
    chosen = (
        lax.broadcasted_iota(jnp.int32, (embed_ref.shape[0], rows), 0) == type_ref[...]
    ).astype(jnp.float32)
    embedded = jnp.dot(
        chosen.T.astype(jnp.bfloat16), embed_ref[...], preferred_element_type=jnp.float32
    )
    home = pack_ref.at[hops]
    home[:rows, :] = (query_ref[...].astype(jnp.float32) + embedded).astype(jnp.bfloat16)
    within = promoter_ref[...] + offset_ref[...] - position * bins
    high = lax.shift_right_arithmetic(within, 8)
    digit = lax.broadcasted_iota(jnp.int32, (EXTRA, rows), 0)
    corner = jnp.where(digit == 0, high, within - 256 * high).astype(jnp.float32)
    home[rows:, :] = jnp.zeros((EXTRA, width), jnp.bfloat16)
    home[rows:, :rows] = corner.astype(jnp.bfloat16)

    around = jnp.minimum(position, hops) + jnp.minimum(seq_count - 1 - position, hops)
    pl.semaphore_wait(barrier, around + head_count - 1)

    side = 1 - 2 * lax.rem(position, 2)
    partner = position + side

    def query_copy(source, slot, target, send):
        return pltpu.make_async_remote_copy(
            src_ref=pack_ref.at[source], dst_ref=pack_ref.at[slot], send_sem=q_send.at[send],
            recv_sem=q_recv.at[slot], device_id=(target, mine), device_id_type=MESH,
        )

    sends = [
        (True, lambda: query_copy(hops, hops + side, partner, 0)),
        (inside(position + 2), lambda: query_copy(hops, hops + 2, position + 2, 1)),
        (inside(position - 2), lambda: query_copy(hops, hops - 2, position - 2, 2)),
    ]
    onward, final = [], []
    for s, send in ((1, 3), (-1, 5)):
        onward += [
            (
                inside(position - 2 * s) & inside(position + 2 * s),
                lambda s=s, send=send: query_copy(
                    hops + 2 * s, hops + 4 * s, position + 2 * s, send
                ),
            ),
            (
                inside(position - 2 * s),
                lambda s=s, send=send: query_copy(
                    hops + 2 * s, hops + 2 * s + side, partner, send + 1
                ),
            ),
        ]
        final.append(
            (
                inside(position - 4 * s) & (side == -s),
                lambda s=s: query_copy(hops + 4 * s, hops + 3 * s, partner, 7),
            )
        )

    def each(entries, act):
        for condition, make in entries:
            if condition is True:
                act(make())
            else:

                @pl.when(condition)
                def _(make=make):
                    act(make())

    def arrived(d):
        @pl.when(inside(position - d))
        def _():
            query_copy(hops, d + hops, partner, 0).wait_recv()

    def out_copy(slot, target):
        return pltpu.make_async_remote_copy(
            src_ref=out_ref.at[slot], dst_ref=back_ref.at[slot], send_sem=o_send.at[slot],
            recv_sem=o_recv.at[slot], device_id=(target, mine), device_id_type=MESH,
        )

    def stat_copy(slot, target):
        return pltpu.make_async_remote_copy(
            src_ref=stat_ref.at[slot], dst_ref=back_stat_ref.at[slot], send_sem=s_send.at[slot],
            recv_sem=s_recv.at[slot], device_id=(target, mine), device_id_type=MESH,
        )

    each(sends, lambda copy: copy.start())

    for d in offsets:

        @pl.when(jnp.logical_not(inside(position - d)))
        def _(d=d):
            pack_ref[d + hops] = jnp.zeros((rows + EXTRA, width), jnp.bfloat16)

    def run(columns, slots):
        attend(
            columns, slots, pack_ref, keys_ref, values_ref, slope_ref, score_ref, out_ref, stat_ref
        )

    def give(d):
        @pl.when(inside(position - d))
        def _():
            stat_copy(d + hops, position - d).start()
            out_copy(d + hops, position - d).start()

    loads[0].wait()
    prepare_keys(k_ref, keys_ref)
    loads[1].wait()
    prepare_values(v_ref, values_ref)
    run([(0, 1)], [hops])
    arrived(2)
    arrived(-2)
    each(onward, lambda copy: copy.start())
    for hop in (2, 1, 4, 3):
        if hop == 1:
            arrived(4)
            arrived(-4)
            each(final, lambda copy: copy.start())
        if hop in (1, 3):
            for d in (hop, -hop):
                arrived(d)
        if hop == 4:
            for d in (hop, -hop):

                @pl.when(inside(position - d))
                def _(d=d):
                    run([(abs(d), 1 if d > 0 else -1)], [d + hops])
        else:
            run([(hop, 1), (hop, -1)], [hop + hops, hops - hop])
        for d in (hop, -hop):
            give(d)

    back_stat_ref[hops] = stat_ref[hops]
    for d in offsets:
        slot = d + hops

        @pl.when(inside(position + d))
        def _(d=d, slot=slot):
            stat_copy(slot, position + d).wait_recv()

        @pl.when(jnp.logical_not(inside(position + d)))
        def _(slot=slot):
            back_stat_ref[slot, :groups, :] = jnp.full((groups, rows), FAR, jnp.float32)
            back_stat_ref[slot, groups:, :] = jnp.zeros((groups, rows), jnp.float32)

    slots = 2 * hops + 1
    peak = back_stat_ref[0, :groups, :]
    for slot in range(1, slots):
        peak = jnp.maximum(peak, back_stat_ref[slot, :groups, :])
    factors = [jnp.exp2(back_stat_ref[slot, :groups, :] - peak) for slot in range(slots)]
    total = factors[0] * back_stat_ref[0, groups:, :]
    for slot in range(1, slots):
        total = total + factors[slot] * back_stat_ref[slot, groups:, :]

    def scaled(part, factor):
        part = part.astype(jnp.float32)
        pieces = [
            part[head * HEAD_DIM : (head + 1) * HEAD_DIM] * factor[head : head + 1]
            for head in range(groups)
        ]
        return jnp.concatenate(pieces, axis=0)

    sum_ref[...] = scaled(out_ref[hops], factors[hops] / total)
    for d in offsets:
        slot = d + hops

        @pl.when(inside(position + d))
        def _(d=d, slot=slot):
            out_copy(slot, position + d).wait_recv()
            sum_ref[...] += scaled(back_ref[slot], factors[slot] / total)

    pooled = sum_ref[...].T.astype(jnp.bfloat16)
    loads[2].wait()

    def head_copy(r, target):
        return pltpu.make_async_remote_copy(
            src_ref=part_ref.at[r - 1], dst_ref=head_ref.at[r - 1], send_sem=h_send.at[r - 1],
            recv_sem=h_recv.at[r - 1], device_id=(position, target), device_id_type=MESH,
        )

    def share(target):
        columns = pl.ds(pl.multiple_of(target * piece, piece), piece)
        return jnp.dot(pooled, w_ref[:, columns], preferred_element_type=jnp.float32)

    for r in range(1, head_count):
        target = lax.rem(mine + r, head_count)
        part_ref[r - 1] = share(target).astype(jnp.bfloat16)
        head_copy(r, target).start()
    result = share(mine)
    for r in range(1, head_count):
        head_copy(r, lax.rem(mine + r, head_count)).wait_recv()
        result = result + head_ref[r - 1].astype(jnp.float32)
    result_ref[...] = result

    each(sends + onward + final, lambda copy: copy.wait_send())
    for r in range(1, head_count):
        head_copy(r, lax.rem(mine + r, head_count)).wait_send()
    for d in offsets:

        @pl.when(inside(position - d))
        def _(d=d):
            stat_copy(d + hops, position - d).wait_send()
            out_copy(d + hops, position - d).wait_send()


def local(queries, cell_types, promoters, offsets, cell_embed, bin_keys, bin_values, slopes, w_out):
    seq_count = lax.axis_size("seq")
    bins = bin_keys.shape[0]
    rows, width = queries.shape
    groups = slopes.shape[0]
    hops = min(HOPS, seq_count - 1)
    head_count = lax.axis_size("head")
    slots = 2 * hops + 1
    piece = w_out.shape[1] // head_count
    vmem = pl.BlockSpec(memory_space=pltpu.VMEM)
    anywhere = pl.BlockSpec(memory_space=pl.ANY)
    result = pl.pallas_call(
        functools.partial(attend_kernel, hops, seq_count, head_count),
        out_shape=jax.ShapeDtypeStruct((rows, piece), jnp.float32),
        in_specs=[vmem] * 5 + [anywhere] * 3 + [pl.BlockSpec(memory_space=pltpu.SMEM)],
        out_specs=vmem,
        scratch_shapes=[
            pltpu.VMEM((bins, width), jnp.bfloat16),
            pltpu.VMEM((bins, width), jnp.bfloat16),
            pltpu.VMEM((groups, bins, LANES), jnp.bfloat16),
            pltpu.VMEM((width, bins), jnp.bfloat16),
            pltpu.VMEM(w_out.shape, jnp.bfloat16),
            pltpu.VMEM((slots, rows + EXTRA, width), jnp.bfloat16),
            pltpu.VMEM((slots, width, rows), jnp.bfloat16),
            pltpu.VMEM((slots, 2 * groups, rows), jnp.float32),
            pltpu.VMEM((slots, width, rows), jnp.bfloat16),
            pltpu.VMEM((slots, 2 * groups, rows), jnp.float32),
            pltpu.VMEM((2, bins, 2 * rows), jnp.float32),
            pltpu.VMEM((width, rows), jnp.float32),
            pltpu.VMEM((head_count - 1, rows, piece), jnp.bfloat16),
            pltpu.VMEM((head_count - 1, rows, piece), jnp.bfloat16),
            pltpu.SemaphoreType.DMA((3,)),
        ]
        + [pltpu.SemaphoreType.DMA((slots,))] * 6
        + [pltpu.SemaphoreType.DMA((head_count - 1,))] * 2,
        compiler_params=pltpu.CompilerParams(collective_id=0, has_side_effects=True),
    )(
        queries,
        cell_types[None],
        promoters[None],
        offsets[None],
        cell_embed,
        bin_keys,
        bin_values,
        w_out,
        slopes,
    )
    return result.astype(jnp.bfloat16)


def solution(mesh):
    return jax.shard_map(
        local,
        mesh=mesh,
        in_specs=(
            P("seq", "head"),
            P("seq"),
            P("seq"),
            P("seq"),
            P(None, "head"),
            P("seq", "head"),
            P("seq", "head"),
            P("head"),
            P("head", None),
        ),
        out_specs=P("seq", "head"),
        check_vma=False,
    )
```

```python
import functools

import jax
import jax.numpy as jnp
from jax import lax
from jax.experimental import pallas as pl
from jax.experimental.pallas import tpu as pltpu
from jax.sharding import PartitionSpec as P

HEAD_DIM = 96
RADIUS = 7812
SHIFT = 64
HOPS = 4
LANES = 128
CHUNK = 256
EXTRA = 16
LOG2E = 1.4426950408889634
FAR = -1e30
PIECES = 2


MESH = pl.DeviceIdType.MESH


def placed(head):
    tile, offset = divmod(head * HEAD_DIM, LANES)
    return tile, offset, (offset + HEAD_DIM) % LANES


def spare_lanes(shape, free):
    lane = lax.broadcasted_iota(jnp.int32, shape, len(shape) - 1) - free
    return lane, (lane >= 0) & (lane < LANES - HEAD_DIM)


def head_tile(tile_at, head):
    tile, offset, _ = placed(head)
    own = tile_at(tile)
    if offset + HEAD_DIM > LANES:
        other = tile_at(tile + 1)
        lane = lax.broadcasted_iota(jnp.int32, own.shape, 1)
        own = jnp.where(lane >= offset, own, other)
    return own


def prepare_keys(k_ref, keys_ref):
    for begin in range(0, k_ref.shape[0], CHUNK):
        index = lax.broadcasted_iota(jnp.int32, (CHUNK, LANES), 0) + begin
        for head in range(keys_ref.shape[0]):
            _, _, free = placed(head)
            lane, inner = spare_lanes((CHUNK, LANES), free)
            part = jnp.where(lane % 2 == 0, index // 256, index % 256)
            part = part.astype(jnp.float32).astype(jnp.bfloat16)
            tile = head_tile(
                lambda t: k_ref[begin : begin + CHUNK, t * LANES : (t + 1) * LANES], head
            )
            keys_ref[head, begin : begin + CHUNK, :] = jnp.where(inner, part, tile)


def prepare_values(v_ref, values_ref):
    for begin in range(0, v_ref.shape[0], CHUNK):
        turned = v_ref[begin : begin + CHUNK, :].astype(jnp.float32).T.astype(jnp.bfloat16)
        values_ref[:, begin : begin + CHUNK] = turned


def prepare_query(tile_at, head, slope, sign):
    _, _, free = placed(head)
    scaled = head_tile(tile_at, head).astype(jnp.float32) * (LOG2E * HEAD_DIM**-0.5)
    high = scaled.astype(jnp.bfloat16)
    low = (scaled - high.astype(jnp.float32)).astype(jnp.bfloat16)
    bias = jnp.full((1, LANES), slope * -sign, jnp.float32)
    first = bias.astype(jnp.bfloat16).astype(jnp.float32)
    second = (bias - first).astype(jnp.bfloat16).astype(jnp.float32)
    third = (bias - first - second).astype(jnp.bfloat16).astype(jnp.float32)
    lane, _ = spare_lanes((1, LANES), free)
    weight = jnp.where(lane % 2 == 0, 256.0, 1.0)
    near, far = (lane >= 0) & (lane < 2), (lane >= 2) & (lane < 4)
    upper = jnp.where(near, first, jnp.where(far, second, 0.0)) * weight
    lower = jnp.where(near, third, 0.0) * weight
    _, inner = spare_lanes(scaled.shape, free)
    high = jnp.where(inner, upper.astype(jnp.bfloat16), high)
    low = jnp.where(inner, lower.astype(jnp.bfloat16), low)
    return jnp.concatenate([high, low], axis=1)


def attend(
    columns, slots, after, pack_ref, keys_ref, values_ref, slope_ref, score_ref, out_ref, stat_ref
):
    groups, bins, _ = keys_ref.shape
    rows = out_ref.shape[2]
    within = []
    for slot in slots:
        corner = pack_ref[slot, :EXTRA, :rows].astype(jnp.float32)
        within.append(corner[0:1] * 256.0 + corner[1:2])
    aheads = [hop * bins - sign * inside for (hop, sign), inside in zip(columns, within)]
    first, last = bins, 0
    for begin in range(0, bins, CHUNK):
        for hop, sign in columns:
            nearest = hop * bins + (begin - bins + 1 if sign > 0 else 1 - begin - CHUNK) - SHIFT
            if hop < 2 or nearest <= RADIUS:
                first, last = min(first, begin), max(last, begin + CHUNK)
    sublane = lax.broadcasted_iota(jnp.int32, (8, rows), 0).astype(jnp.float32)

    def biased(column, start, slope, score):
        hop, sign = columns[column]
        index = sublane + float(start)
        if hop == 0 or (hop == 1 and (start < SHIFT if sign > 0 else start + 8 > bins - SHIFT)):
            before = jnp.maximum(-(index * sign + aheads[column]), 0.0)
            score = score - (2.0 * slope) * before
        farthest = hop * bins + (start + 7 if sign > 0 else bins - 1 - start) + SHIFT
        if farthest > RADIUS:
            score = jnp.where(index * sign <= RADIUS - aheads[column], score, FAR)
        return score

    def scores(head):
        slope = slope_ref[head] * LOG2E
        query = [
            prepare_query(
                lambda t: pack_ref[slot, EXTRA + t * rows : EXTRA + (t + 1) * rows, :],
                head, slope, float(sign),
            )
            for slot, (hop, sign) in zip(slots, columns)
        ]
        query = jnp.concatenate(query, axis=0) if len(slots) > 1 else query[0]
        tops = [None] * len(slots)
        for begin in range(first, last, CHUNK):
            keys = keys_ref[head, begin : begin + CHUNK, :]
            raw = lax.dot_general(
                jnp.concatenate([keys, keys], axis=1),
                query,
                (((1,), (1,)), ((), ())),
                preferred_element_type=jnp.float32,
            )
            for start in range(0, CHUNK, 8):
                for i in range(len(slots)):
                    lanes = slice(i * rows, (i + 1) * rows)
                    score = biased(i, begin + start, slope, raw[start : start + 8, lanes])
                    score_ref[head % 2, begin + start : begin + start + 8, lanes] = score
                    tops[i] = score if tops[i] is None else jnp.maximum(tops[i], score)
        return [jnp.maximum(jnp.max(top, axis=0, keepdims=True), 0.1 * FAR) for top in tops]

    def pool(head, peaks):
        totals = [None] * len(slots)
        weights = []
        for begin in range(first, last, CHUNK):
            parts = []
            for i in range(len(slots)):
                lanes = slice(i * rows, (i + 1) * rows)
                exps = jnp.exp2(score_ref[head % 2, begin : begin + CHUNK, lanes] - peaks[i])
                total = jnp.sum(exps.reshape(CHUNK // 8, 8, rows), axis=0)
                totals[i] = total if totals[i] is None else totals[i] + total
                parts.append(exps.astype(jnp.bfloat16))
            weights.append(jnp.concatenate(parts, axis=1) if len(slots) > 1 else parts[0])
        gained = jnp.dot(
            values_ref[head * HEAD_DIM : (head + 1) * HEAD_DIM, first:last],
            jnp.concatenate(weights, axis=0),
            preferred_element_type=jnp.float32,
        )
        slope = slope_ref[head] * LOG2E
        for i, slot in enumerate(slots):
            out_ref[slot, head * HEAD_DIM : (head + 1) * HEAD_DIM, :] = gained[
                :, i * rows : (i + 1) * rows
            ].astype(jnp.bfloat16)
            stat_ref[slot, head : head + 1, :] = peaks[i] - slope * aheads[i]
            stat_ref[slot, groups + head : groups + head + 1, :] = jnp.sum(
                totals[i], axis=0, keepdims=True
            )

    peaks = scores(0)
    for head in range(groups):
        later = scores(head + 1) if head + 1 < groups else None
        pool(head, peaks)
        peaks = later
        after(head)


def attend_kernel(
    hops, seq_count, head_count,
    query_ref, type_ref, promoter_ref, offset_ref, embed_ref, k_hbm, v_hbm, w_hbm, slope_ref,
    result_ref,
    k_ref, v_ref, keys_ref, values_ref, w_ref, pack_ref, out_ref, stat_ref, back_ref, back_stat_ref,
    score_ref, sum_ref, part_ref, head_ref,
    load_sem, q_send, q_recv, o_send, o_recv, s_send, s_recv, h_send, h_recv,
):
    position = lax.axis_index("seq")
    mine = lax.axis_index("head")
    width, rows = out_ref.shape[1:]
    groups = width // HEAD_DIM
    piece = result_ref.shape[1]
    loads = [
        pltpu.make_async_copy(src, dst, load_sem.at[i])
        for i, (src, dst) in enumerate(((k_hbm, k_ref), (v_hbm, v_ref), (w_hbm, w_ref)))
    ]
    for load in loads:
        load.start()

    def inside(index):
        return (index >= 0) & (index < seq_count)

    barrier = pltpu.get_barrier_semaphore()
    offsets = [sign * hop for hop in range(1, hops + 1) for sign in (1, -1)]
    for d in offsets:

        @pl.when(inside(position + d))
        def _(d=d):
            pl.semaphore_signal(
                barrier, inc=1, device_id=(position + d, mine), device_id_type=MESH
            )

    for r in range(1, head_count):
        pl.semaphore_signal(
            barrier, inc=1, device_id=(position, lax.rem(mine + r, head_count)), device_id_type=MESH
        )

    bins = k_ref.shape[0]
    chosen = (
        lax.broadcasted_iota(jnp.int32, (embed_ref.shape[0], rows), 0) == type_ref[...]
    ).astype(jnp.float32)
    embedded = jnp.dot(
        chosen.T.astype(jnp.bfloat16), embed_ref[...], preferred_element_type=jnp.float32
    )
    home = pack_ref.at[hops]
    query = (query_ref[...].astype(jnp.float32) + embedded).astype(jnp.bfloat16)
    for tile in range(width // LANES):
        home[EXTRA + tile * rows : EXTRA + (tile + 1) * rows, :] = query[
            :, tile * LANES : (tile + 1) * LANES
        ]
    within = promoter_ref[...] + offset_ref[...] - position * bins
    high = lax.shift_right_arithmetic(within, 8)
    digit = lax.broadcasted_iota(jnp.int32, (EXTRA, rows), 0)
    corner = jnp.where(digit == 0, high, within - 256 * high).astype(jnp.float32)
    home[:EXTRA, :] = corner.astype(jnp.bfloat16)

    around = jnp.minimum(position, hops) + jnp.minimum(seq_count - 1 - position, hops)
    pl.semaphore_wait(barrier, around + head_count - 1)

    side = 1 - 2 * lax.rem(position, 2)
    partner = position + side

    length = pack_ref.shape[1]
    cuts = [0, EXTRA + (length - EXTRA) // 2, length]

    def query_copy(source, slot, target, send, k):
        part = slice(cuts[k], cuts[k + 1])
        return pltpu.make_async_remote_copy(
            src_ref=pack_ref.at[source, part], dst_ref=pack_ref.at[slot, part],
            send_sem=q_send.at[send, k], recv_sem=q_recv.at[slot, k],
            device_id=(target, mine), device_id_type=MESH,
        )

    sends = [
        (True, lambda k: query_copy(hops, hops + side, partner, 0, k)),
        (inside(position + 2), lambda k: query_copy(hops, hops + 2, position + 2, 1, k)),
        (inside(position - 2), lambda k: query_copy(hops, hops - 2, position - 2, 2, k)),
    ]
    onward, across, final = [], [], []
    for s, send in ((1, 3), (-1, 5)):
        onward.append(
            (
                inside(position - 2 * s) & inside(position + 2 * s),
                lambda k, s=s, send=send: query_copy(
                    hops + 2 * s, hops + 4 * s, position + 2 * s, send, k
                ),
            )
        )
        across.append(
            (
                inside(position + 2 * s),
                lambda k, s=s, send=send: query_copy(
                    hops - side, hops + 2 * s - side, position + 2 * s, send + 1, k
                ),
            )
        )
        final.append(
            (
                inside(position - 4 * s) & (side == -s),
                lambda k, s=s: query_copy(hops + 4 * s, hops + 3 * s, partner, 7, k),
            )
        )

    def each(entries, act, k):
        for condition, make in entries:
            if condition is True:
                act(make(k))
            else:

                @pl.when(condition)
                def _(make=make):
                    act(make(k))

    def arrived(d, k):
        @pl.when(inside(position - d) & (side != -d))
        def _():
            query_copy(hops, d + hops, partner, 0, k).wait_recv()

    def out_copy(slot, target, head=None):
        part = slice(0, width)
        if head is not None:
            part = slice(head * HEAD_DIM, (head + 1) * HEAD_DIM)
        return pltpu.make_async_remote_copy(
            src_ref=out_ref.at[slot, part], dst_ref=back_ref.at[slot, part], send_sem=o_send.at[slot],
            recv_sem=o_recv.at[slot], device_id=(target, mine), device_id_type=MESH,
        )

    def stat_copy(slot, target):
        return pltpu.make_async_remote_copy(
            src_ref=stat_ref.at[slot], dst_ref=back_stat_ref.at[slot], send_sem=s_send.at[slot],
            recv_sem=s_recv.at[slot], device_id=(target, mine), device_id_type=MESH,
        )

    for k in range(PIECES):
        each(sends, lambda copy: copy.start(), k)

    for d in offsets:

        @pl.when(jnp.logical_not(inside(position - d)))
        def _(d=d):
            pack_ref[d + hops] = jnp.zeros(pack_ref.shape[1:], jnp.bfloat16)

    def run(columns, slots, after):
        attend(
            columns, slots, after, pack_ref, keys_ref, values_ref, slope_ref, score_ref, out_ref,
            stat_ref,
        )

    def forward(k):
        query_copy(hops, hops - side, partner, 0, k).wait_recv()
        each(across, lambda copy: copy.start(), k)
        arrived(2, k)
        arrived(-2, k)
        each(onward, lambda copy: copy.start(), k)

    def give(ds):
        def after(head):
            for d in ds:

                @pl.when(inside(position - d))
                def _(d=d):
                    if head == groups - 1:
                        stat_copy(d + hops, position - d).start()
                    out_copy(d + hops, position - d, head).start()

        return after

    def between(head):
        if head in (1, 3):
            forward(head // 2)

    loads[0].wait()
    prepare_keys(k_ref, keys_ref)
    loads[1].wait()
    prepare_values(v_ref, values_ref)
    run([(0, 1)], [hops], between)
    run([(2, 1), (2, -1)], [hops + 2, hops - 2], give((2, -2)))
    for k in range(PIECES):
        arrived(4, k)
        arrived(-4, k)
        each(final, lambda copy: copy.start(), k)
    for d in (4, -4):

        @pl.when(inside(position - d))
        def _(d=d):
            run([(4, d // 4)], [d + hops], give((d,)))

    for hop in (1, 3):
        for k in range(PIECES):
            arrived(hop, k)
            arrived(-hop, k)
        run([(hop, 1), (hop, -1)], [hop + hops, hops - hop], give((hop, -hop)))

    back_stat_ref[hops] = stat_ref[hops]
    for d in offsets:
        slot = d + hops

        @pl.when(inside(position + d))
        def _(d=d, slot=slot):
            stat_copy(slot, position + d).wait_recv()

        @pl.when(jnp.logical_not(inside(position + d)))
        def _(slot=slot):
            back_stat_ref[slot, :groups, :] = jnp.full((groups, rows), FAR, jnp.float32)
            back_stat_ref[slot, groups:, :] = jnp.zeros((groups, rows), jnp.float32)

    slots = 2 * hops + 1
    peak = back_stat_ref[0, :groups, :]
    for slot in range(1, slots):
        peak = jnp.maximum(peak, back_stat_ref[slot, :groups, :])
    factors = [jnp.exp2(back_stat_ref[slot, :groups, :] - peak) for slot in range(slots)]
    total = factors[0] * back_stat_ref[0, groups:, :]
    for slot in range(1, slots):
        total = total + factors[slot] * back_stat_ref[slot, groups:, :]

    def scaled(part, factor):
        part = part.astype(jnp.float32)
        pieces = [
            part[head * HEAD_DIM : (head + 1) * HEAD_DIM] * factor[head : head + 1]
            for head in range(groups)
        ]
        return jnp.concatenate(pieces, axis=0)

    sum_ref[...] = scaled(out_ref[hops], factors[hops] / total)
    for d in offsets:
        slot = d + hops

        @pl.when(inside(position + d))
        def _(d=d, slot=slot):
            out_copy(slot, position + d).wait_recv()
            sum_ref[...] += scaled(back_ref[slot], factors[slot] / total)

    pooled = sum_ref[...].T.astype(jnp.bfloat16)
    loads[2].wait()

    def head_copy(r, target):
        return pltpu.make_async_remote_copy(
            src_ref=part_ref.at[r - 1], dst_ref=head_ref.at[r - 1], send_sem=h_send.at[r - 1],
            recv_sem=h_recv.at[r - 1], device_id=(position, target), device_id_type=MESH,
        )

    def share(target):
        columns = pl.ds(pl.multiple_of(target * piece, piece), piece)
        return jnp.dot(pooled, w_ref[:, columns], preferred_element_type=jnp.float32)

    for r in range(1, head_count):
        target = lax.rem(mine + r, head_count)
        part_ref[r - 1] = share(target).astype(jnp.bfloat16)
        head_copy(r, target).start()
    result = share(mine)
    for r in range(1, head_count):
        head_copy(r, lax.rem(mine + r, head_count)).wait_recv()
        result = result + head_ref[r - 1].astype(jnp.float32)
    result_ref[...] = result

    for k in range(PIECES):
        each(sends + onward + across + final, lambda copy: copy.wait_send(), k)
    for r in range(1, head_count):
        head_copy(r, lax.rem(mine + r, head_count)).wait_send()
    for d in offsets:

        @pl.when(inside(position - d))
        def _(d=d):
            stat_copy(d + hops, position - d).wait_send()
            out_copy(d + hops, position - d).wait_send()


def local(queries, cell_types, promoters, offsets, cell_embed, bin_keys, bin_values, slopes, w_out):
    seq_count = lax.axis_size("seq")
    bins = bin_keys.shape[0]
    rows, width = queries.shape
    groups = slopes.shape[0]
    hops = min(HOPS, seq_count - 1)
    head_count = lax.axis_size("head")
    slots = 2 * hops + 1
    piece = w_out.shape[1] // head_count
    vmem = pl.BlockSpec(memory_space=pltpu.VMEM)
    anywhere = pl.BlockSpec(memory_space=pl.ANY)
    result = pl.pallas_call(
        functools.partial(attend_kernel, hops, seq_count, head_count),
        out_shape=jax.ShapeDtypeStruct((rows, piece), jnp.float32),
        in_specs=[vmem] * 5 + [anywhere] * 3 + [pl.BlockSpec(memory_space=pltpu.SMEM)],
        out_specs=vmem,
        scratch_shapes=[
            pltpu.VMEM((bins, width), jnp.bfloat16),
            pltpu.VMEM((bins, width), jnp.bfloat16),
            pltpu.VMEM((groups, bins, LANES), jnp.bfloat16),
            pltpu.VMEM((width, bins), jnp.bfloat16),
            pltpu.VMEM(w_out.shape, jnp.bfloat16),
            pltpu.VMEM((slots, EXTRA + rows * width // LANES, LANES), jnp.bfloat16),
            pltpu.VMEM((slots, width, rows), jnp.bfloat16),
            pltpu.VMEM((slots, 2 * groups, rows), jnp.float32),
            pltpu.VMEM((slots, width, rows), jnp.bfloat16),
            pltpu.VMEM((slots, 2 * groups, rows), jnp.float32),
            pltpu.VMEM((2, bins, 2 * rows), jnp.float32),
            pltpu.VMEM((width, rows), jnp.float32),
            pltpu.VMEM((head_count - 1, rows, piece), jnp.bfloat16),
            pltpu.VMEM((head_count - 1, rows, piece), jnp.bfloat16),
            pltpu.SemaphoreType.DMA((3,)),
        ]
        + [pltpu.SemaphoreType.DMA((slots, PIECES))] * 2
        + [pltpu.SemaphoreType.DMA((slots,))] * 4
        + [pltpu.SemaphoreType.DMA((head_count - 1,))] * 2,
        compiler_params=pltpu.CompilerParams(collective_id=0, has_side_effects=True),
    )(
        queries,
        cell_types[None],
        promoters[None],
        offsets[None],
        cell_embed,
        bin_keys,
        bin_values,
        w_out,
        slopes,
    )
    return result.astype(jnp.bfloat16)


def solution(mesh):
    return jax.shard_map(
        local,
        mesh=mesh,
        in_specs=(
            P("seq", "head"),
            P("seq"),
            P("seq"),
            P("seq"),
            P(None, "head"),
            P("seq", "head"),
            P("seq", "head"),
            P("head"),
            P("head", None),
        ),
        out_specs=P("seq", "head"),
        check_vma=False,
    )
```

```python
import functools

import jax
import jax.numpy as jnp
from jax import lax
from jax.experimental import pallas as pl
from jax.experimental.pallas import tpu as pltpu
from jax.sharding import PartitionSpec as P

HEAD_DIM = 96
RADIUS = 7812
SHIFT = 64
HOPS = 4
LANES = 128
CHUNK = 256
EXTRA = 16
LOG2E = 1.4426950408889634
FAR = -1e30
PIECES = 2


MESH = pl.DeviceIdType.MESH


def placed(head):
    tile, offset = divmod(head * HEAD_DIM, LANES)
    return tile, offset, (offset + HEAD_DIM) % LANES


def spare_lanes(shape, free):
    lane = lax.broadcasted_iota(jnp.int32, shape, len(shape) - 1) - free
    return lane, (lane >= 0) & (lane < LANES - HEAD_DIM)


def head_tile(tile_at, head):
    tile, offset, _ = placed(head)
    own = tile_at(tile)
    if offset + HEAD_DIM > LANES:
        other = tile_at(tile + 1)
        lane = lax.broadcasted_iota(jnp.int32, own.shape, 1)
        own = jnp.where(lane >= offset, own, other)
    return own


def prepare_keys(k_ref, keys_ref):
    for begin in range(0, k_ref.shape[0], CHUNK):
        index = lax.broadcasted_iota(jnp.int32, (CHUNK, LANES), 0) + begin
        for head in range(keys_ref.shape[0]):
            _, _, free = placed(head)
            lane, inner = spare_lanes((CHUNK, LANES), free)
            part = jnp.where(lane % 2 == 0, index // 256, index % 256)
            part = part.astype(jnp.float32).astype(jnp.bfloat16)
            tile = head_tile(
                lambda t: k_ref[begin : begin + CHUNK, t * LANES : (t + 1) * LANES], head
            )
            keys_ref[head, begin : begin + CHUNK, :] = jnp.where(inner, part, tile)


def prepare_values(v_ref, values_ref):
    for begin in range(0, v_ref.shape[0], CHUNK):
        turned = v_ref[begin : begin + CHUNK, :].astype(jnp.float32).T.astype(jnp.bfloat16)
        values_ref[:, begin : begin + CHUNK] = turned


def prepare_query(tile_at, head, slope, sign):
    _, _, free = placed(head)
    scaled = head_tile(tile_at, head).astype(jnp.float32) * (LOG2E * HEAD_DIM**-0.5)
    high = scaled.astype(jnp.bfloat16)
    low = (scaled - high.astype(jnp.float32)).astype(jnp.bfloat16)
    bias = jnp.full((1, LANES), slope * -sign, jnp.float32)
    first = bias.astype(jnp.bfloat16).astype(jnp.float32)
    second = (bias - first).astype(jnp.bfloat16).astype(jnp.float32)
    third = (bias - first - second).astype(jnp.bfloat16).astype(jnp.float32)
    lane, _ = spare_lanes((1, LANES), free)
    weight = jnp.where(lane % 2 == 0, 256.0, 1.0)
    near, far = (lane >= 0) & (lane < 2), (lane >= 2) & (lane < 4)
    upper = jnp.where(near, first, jnp.where(far, second, 0.0)) * weight
    lower = jnp.where(near, third, 0.0) * weight
    _, inner = spare_lanes(scaled.shape, free)
    high = jnp.where(inner, upper.astype(jnp.bfloat16), high)
    low = jnp.where(inner, lower.astype(jnp.bfloat16), low)
    return jnp.concatenate([high, low], axis=1)


def attend(
    columns, slots, after, pack_ref, keys_ref, values_ref, slope_ref, score_ref, out_ref, stat_ref
):
    groups, bins, _ = keys_ref.shape
    rows = out_ref.shape[2]
    within = []
    for slot in slots:
        corner = pack_ref[slot, :EXTRA, :rows].astype(jnp.float32)
        within.append(corner[0:1] * 256.0 + corner[1:2])
    aheads = [hop * bins - sign * inside for (hop, sign), inside in zip(columns, within)]
    first, last = bins, 0
    for begin in range(0, bins, CHUNK):
        for hop, sign in columns:
            nearest = hop * bins + (begin - bins + 1 if sign > 0 else 1 - begin - CHUNK) - SHIFT
            if hop < 2 or nearest <= RADIUS:
                first, last = min(first, begin), max(last, begin + CHUNK)
    sublane = lax.broadcasted_iota(jnp.int32, (8, rows), 0).astype(jnp.float32)

    def biased(column, start, slope, score):
        hop, sign = columns[column]
        index = sublane + float(start)
        if hop == 0 or (hop == 1 and (start < SHIFT if sign > 0 else start + 8 > bins - SHIFT)):
            before = jnp.maximum(-(index * sign + aheads[column]), 0.0)
            score = score - (2.0 * slope) * before
        farthest = hop * bins + (start + 7 if sign > 0 else bins - 1 - start) + SHIFT
        if farthest > RADIUS:
            score = jnp.where(index * sign <= RADIUS - aheads[column], score, FAR)
        return score

    def scores(head):
        slope = slope_ref[head] * LOG2E
        query = [
            prepare_query(
                lambda t: pack_ref[slot, EXTRA + t * rows : EXTRA + (t + 1) * rows, :],
                head, slope, float(sign),
            )
            for slot, (hop, sign) in zip(slots, columns)
        ]
        query = jnp.concatenate(query, axis=0) if len(slots) > 1 else query[0]
        tops = [None] * len(slots)
        for begin in range(first, last, CHUNK):
            keys = keys_ref[head, begin : begin + CHUNK, :]
            raw = lax.dot_general(
                jnp.concatenate([keys, keys], axis=1),
                query,
                (((1,), (1,)), ((), ())),
                preferred_element_type=jnp.float32,
            )
            for start in range(0, CHUNK, 8):
                for i in range(len(slots)):
                    lanes = slice(i * rows, (i + 1) * rows)
                    score = biased(i, begin + start, slope, raw[start : start + 8, lanes])
                    score_ref[head % 2, begin + start : begin + start + 8, lanes] = score
                    tops[i] = score if tops[i] is None else jnp.maximum(tops[i], score)
        return [jnp.maximum(jnp.max(top, axis=0, keepdims=True), 0.1 * FAR) for top in tops]

    def pool(head, peaks):
        totals = [None] * len(slots)
        weights = []
        for begin in range(first, last, CHUNK):
            parts = []
            for i in range(len(slots)):
                lanes = slice(i * rows, (i + 1) * rows)
                exps = jnp.exp2(score_ref[head % 2, begin : begin + CHUNK, lanes] - peaks[i])
                total = jnp.sum(exps.reshape(CHUNK // 8, 8, rows), axis=0)
                totals[i] = total if totals[i] is None else totals[i] + total
                parts.append(exps.astype(jnp.bfloat16))
            weights.append(jnp.concatenate(parts, axis=1) if len(slots) > 1 else parts[0])
        gained = jnp.dot(
            values_ref[head * HEAD_DIM : (head + 1) * HEAD_DIM, first:last],
            jnp.concatenate(weights, axis=0),
            preferred_element_type=jnp.float32,
        )
        slope = slope_ref[head] * LOG2E
        for i, slot in enumerate(slots):
            out_ref[slot, head * HEAD_DIM : (head + 1) * HEAD_DIM, :] = gained[
                :, i * rows : (i + 1) * rows
            ].astype(jnp.bfloat16)
            stat_ref[slot, head : head + 1, :] = peaks[i] - slope * aheads[i]
            stat_ref[slot, groups + head : groups + head + 1, :] = jnp.sum(
                totals[i], axis=0, keepdims=True
            )

    peaks = scores(0)
    for head in range(groups):
        later = scores(head + 1) if head + 1 < groups else None
        pool(head, peaks)
        peaks = later
        after(head)


def attend_kernel(
    hops, seq_count, head_count,
    query_ref, type_ref, promoter_ref, offset_ref, embed_ref, k_hbm, v_hbm, w_hbm, slope_ref,
    result_ref,
    k_ref, v_ref, keys_ref, values_ref, w_ref, pack_ref, out_ref, stat_ref, back_ref, back_stat_ref,
    score_ref, sum_ref, part_ref, head_ref,
    load_sem, q_send, q_recv, o_send, o_recv, s_send, s_recv, h_send, h_recv,
):
    position = lax.axis_index("seq")
    mine = lax.axis_index("head")
    width, rows = out_ref.shape[1:]
    groups = width // HEAD_DIM
    piece = result_ref.shape[1]
    loads = [
        pltpu.make_async_copy(src, dst, load_sem.at[i])
        for i, (src, dst) in enumerate(((k_hbm, k_ref), (v_hbm, v_ref), (w_hbm, w_ref)))
    ]
    for load in loads:
        load.start()

    def inside(index):
        return (index >= 0) & (index < seq_count)

    barrier = pltpu.get_barrier_semaphore()
    offsets = [sign * hop for hop in range(1, hops + 1) for sign in (1, -1)]
    for d in offsets:

        @pl.when(inside(position + d))
        def _(d=d):
            pl.semaphore_signal(
                barrier, inc=1, device_id=(position + d, mine), device_id_type=MESH
            )

    for r in range(1, head_count):
        pl.semaphore_signal(
            barrier, inc=1, device_id=(position, lax.rem(mine + r, head_count)), device_id_type=MESH
        )

    bins = k_ref.shape[0]
    chosen = (
        lax.broadcasted_iota(jnp.int32, (embed_ref.shape[0], rows), 0) == type_ref[...]
    ).astype(jnp.float32)
    embedded = jnp.dot(
        chosen.T.astype(jnp.bfloat16), embed_ref[...], preferred_element_type=jnp.float32
    )
    home = pack_ref.at[hops]
    query = (query_ref[...].astype(jnp.float32) + embedded).astype(jnp.bfloat16)
    for tile in range(width // LANES):
        home[EXTRA + tile * rows : EXTRA + (tile + 1) * rows, :] = query[
            :, tile * LANES : (tile + 1) * LANES
        ]
    within = promoter_ref[...] + offset_ref[...] - position * bins
    high = lax.shift_right_arithmetic(within, 8)
    digit = lax.broadcasted_iota(jnp.int32, (EXTRA, rows), 0)
    corner = jnp.where(digit == 0, high, within - 256 * high).astype(jnp.float32)
    home[:EXTRA, :] = corner.astype(jnp.bfloat16)

    around = jnp.minimum(position, hops) + jnp.minimum(seq_count - 1 - position, hops)
    pl.semaphore_wait(barrier, around + head_count - 1)

    side = 1 - 2 * lax.rem(position, 2)
    partner = position + side

    length = pack_ref.shape[1]
    cuts = [0, EXTRA + (length - EXTRA) // 2, length]

    def query_copy(source, slot, target, send, k):
        part = slice(cuts[k], cuts[k + 1])
        return pltpu.make_async_remote_copy(
            src_ref=pack_ref.at[source, part], dst_ref=pack_ref.at[slot, part],
            send_sem=q_send.at[send, k], recv_sem=q_recv.at[slot, k],
            device_id=(target, mine), device_id_type=MESH,
        )

    sends = [
        (True, lambda k: query_copy(hops, hops + side, partner, 0, k)),
        (inside(position + 2), lambda k: query_copy(hops, hops + 2, position + 2, 1, k)),
        (inside(position - 2), lambda k: query_copy(hops, hops - 2, position - 2, 2, k)),
    ]
    onward, final = [], []
    for s, send in ((1, 3), (-1, 5)):
        onward += [
            (
                inside(position - 2 * s) & inside(position + 2 * s),
                lambda k, s=s, send=send: query_copy(
                    hops + 2 * s, hops + 4 * s, position + 2 * s, send, k
                ),
            ),
            (
                inside(position - 2 * s),
                lambda k, s=s, send=send: query_copy(
                    hops + 2 * s, hops + 2 * s + side, partner, send + 1, k
                ),
            ),
        ]
        final.append(
            (
                inside(position - 4 * s) & (side == -s),
                lambda k, s=s: query_copy(hops + 4 * s, hops + 3 * s, partner, 7, k),
            )
        )

    def each(entries, act, k):
        for condition, make in entries:
            if condition is True:
                act(make(k))
            else:

                @pl.when(condition)
                def _(make=make):
                    act(make(k))

    def arrived(d, k):
        @pl.when(inside(position - d))
        def _():
            query_copy(hops, d + hops, partner, 0, k).wait_recv()

    def out_copy(slot, target, head=None):
        part = slice(0, width)
        if head is not None:
            part = slice(head * HEAD_DIM, (head + 1) * HEAD_DIM)
        return pltpu.make_async_remote_copy(
            src_ref=out_ref.at[slot, part], dst_ref=back_ref.at[slot, part], send_sem=o_send.at[slot],
            recv_sem=o_recv.at[slot], device_id=(target, mine), device_id_type=MESH,
        )

    def stat_copy(slot, target):
        return pltpu.make_async_remote_copy(
            src_ref=stat_ref.at[slot], dst_ref=back_stat_ref.at[slot], send_sem=s_send.at[slot],
            recv_sem=s_recv.at[slot], device_id=(target, mine), device_id_type=MESH,
        )

    for k in range(PIECES):
        each(sends, lambda copy: copy.start(), k)

    for d in offsets:

        @pl.when(jnp.logical_not(inside(position - d)))
        def _(d=d):
            pack_ref[d + hops] = jnp.zeros(pack_ref.shape[1:], jnp.bfloat16)

    def run(columns, slots, after):
        attend(
            columns, slots, after, pack_ref, keys_ref, values_ref, slope_ref, score_ref, out_ref,
            stat_ref,
        )

    def forward(k):
        arrived(2, k)
        arrived(-2, k)
        each(onward, lambda copy: copy.start(), k)

    def give(ds):
        def after(head):
            for d in ds:

                @pl.when(inside(position - d))
                def _(d=d):
                    if head == groups - 1:
                        stat_copy(d + hops, position - d).start()
                    out_copy(d + hops, position - d, head).start()

        return after

    def between(head):
        if head in (1, 3):
            forward(head // 2)

    loads[0].wait()
    prepare_keys(k_ref, keys_ref)
    loads[1].wait()
    prepare_values(v_ref, values_ref)
    run([(0, 1)], [hops], between)
    run([(2, 1), (2, -1)], [hops + 2, hops - 2], give((2, -2)))
    for k in range(PIECES):
        arrived(4, k)
        arrived(-4, k)
        each(final, lambda copy: copy.start(), k)
    for d in (4, -4):

        @pl.when(inside(position - d))
        def _(d=d):
            run([(4, d // 4)], [d + hops], give((d,)))

    for hop in (1, 3):
        for k in range(PIECES):
            arrived(hop, k)
            arrived(-hop, k)
        run([(hop, 1), (hop, -1)], [hop + hops, hops - hop], give((hop, -hop)))

    back_stat_ref[hops] = stat_ref[hops]
    for d in offsets:
        slot = d + hops

        @pl.when(inside(position + d))
        def _(d=d, slot=slot):
            stat_copy(slot, position + d).wait_recv()

        @pl.when(jnp.logical_not(inside(position + d)))
        def _(slot=slot):
            back_stat_ref[slot, :groups, :] = jnp.full((groups, rows), FAR, jnp.float32)
            back_stat_ref[slot, groups:, :] = jnp.zeros((groups, rows), jnp.float32)

    slots = 2 * hops + 1
    peak = back_stat_ref[0, :groups, :]
    for slot in range(1, slots):
        peak = jnp.maximum(peak, back_stat_ref[slot, :groups, :])
    factors = [jnp.exp2(back_stat_ref[slot, :groups, :] - peak) for slot in range(slots)]
    total = factors[0] * back_stat_ref[0, groups:, :]
    for slot in range(1, slots):
        total = total + factors[slot] * back_stat_ref[slot, groups:, :]

    def scaled(part, factor):
        part = part.astype(jnp.float32)
        pieces = [
            part[head * HEAD_DIM : (head + 1) * HEAD_DIM] * factor[head : head + 1]
            for head in range(groups)
        ]
        return jnp.concatenate(pieces, axis=0)

    sum_ref[...] = scaled(out_ref[hops], factors[hops] / total)
    for d in offsets:
        slot = d + hops

        @pl.when(inside(position + d))
        def _(d=d, slot=slot):
            out_copy(slot, position + d).wait_recv()
            sum_ref[...] += scaled(back_ref[slot], factors[slot] / total)

    pooled = sum_ref[...].T.astype(jnp.bfloat16)
    loads[2].wait()

    chips = head_count // 2
    core = lax.rem(mine, 2)
    twin = mine + 1 - 2 * core
    half = rows // 2

    def head_copy(n, target):
        return pltpu.make_async_remote_copy(
            src_ref=part_ref.at[n], dst_ref=head_ref.at[n], send_sem=h_send.at[n],
            recv_sem=h_recv.at[n], device_id=(position, target), device_id_type=MESH,
        )

    exchanged = []

    def pass_on(n, value, target):
        part_ref[n] = value.astype(jnp.bfloat16)
        exchanged.append((n, target))
        head_copy(n, target).start()

    def taken(n):
        head_copy(n, twin).wait_recv()
        return head_ref[n].astype(jnp.float32)

    def share(target):
        columns = pl.ds(pl.multiple_of(target * piece, piece), piece)
        return jnp.dot(pooled, w_ref[:, columns], preferred_element_type=jnp.float32)

    def elsewhere(k, which):
        return lax.rem(mine - core + 2 * k, head_count) + which

    kept = []
    for k in range(1, chips):
        base = 4 * (k - 1)
        value = share(elsewhere(k, 1 - core))
        pass_on(base + 2, value[half:], twin)
        pass_on(base + 1, value[:half], elsewhere(k, 1 - core))
        value = share(elsewhere(k, core))
        pass_on(base, value[:half], elsewhere(k, core))
        kept.append(value[half:])
    last = 4 * (chips - 1)
    value = share(twin)
    pass_on(last, value[:half], twin)
    pass_on(last + 1, value[half:], twin)
    for k in range(1, chips):
        base = 4 * (k - 1)
        pass_on(base + 3, kept[k - 1] + taken(base + 2), elsewhere(k, core))
    result = share(mine)
    upper = result[:half] + taken(last)
    lower = result[half:] + taken(last + 1)
    for k in range(1, chips):
        base = 4 * (k - 1)
        upper = upper + taken(base) + taken(base + 1)
        lower = lower + taken(base + 3)
    result_ref[:half, :] = upper
    result_ref[half:, :] = lower

    for k in range(PIECES):
        each(sends + onward + final, lambda copy: copy.wait_send(), k)
    for n, target in exchanged:
        head_copy(n, target).wait_send()
    for d in offsets:

        @pl.when(inside(position - d))
        def _(d=d):
            stat_copy(d + hops, position - d).wait_send()
            out_copy(d + hops, position - d).wait_send()


def local(queries, cell_types, promoters, offsets, cell_embed, bin_keys, bin_values, slopes, w_out):
    seq_count = lax.axis_size("seq")
    bins = bin_keys.shape[0]
    rows, width = queries.shape
    groups = slopes.shape[0]
    hops = min(HOPS, seq_count - 1)
    head_count = lax.axis_size("head")
    slots = 2 * hops + 1
    piece = w_out.shape[1] // head_count
    vmem = pl.BlockSpec(memory_space=pltpu.VMEM)
    anywhere = pl.BlockSpec(memory_space=pl.ANY)
    result = pl.pallas_call(
        functools.partial(attend_kernel, hops, seq_count, head_count),
        out_shape=jax.ShapeDtypeStruct((rows, piece), jnp.float32),
        in_specs=[vmem] * 5 + [anywhere] * 3 + [pl.BlockSpec(memory_space=pltpu.SMEM)],
        out_specs=vmem,
        scratch_shapes=[
            pltpu.VMEM((bins, width), jnp.bfloat16),
            pltpu.VMEM((bins, width), jnp.bfloat16),
            pltpu.VMEM((groups, bins, LANES), jnp.bfloat16),
            pltpu.VMEM((width, bins), jnp.bfloat16),
            pltpu.VMEM(w_out.shape, jnp.bfloat16),
            pltpu.VMEM((slots, EXTRA + rows * width // LANES, LANES), jnp.bfloat16),
            pltpu.VMEM((slots, width, rows), jnp.bfloat16),
            pltpu.VMEM((slots, 2 * groups, rows), jnp.float32),
            pltpu.VMEM((slots, width, rows), jnp.bfloat16),
            pltpu.VMEM((slots, 2 * groups, rows), jnp.float32),
            pltpu.VMEM((2, bins, 2 * rows), jnp.float32),
            pltpu.VMEM((width, rows), jnp.float32),
            pltpu.VMEM((2 * head_count - 2, rows // 2, piece), jnp.bfloat16),
            pltpu.VMEM((2 * head_count - 2, rows // 2, piece), jnp.bfloat16),
            pltpu.SemaphoreType.DMA((3,)),
        ]
        + [pltpu.SemaphoreType.DMA((slots, PIECES))] * 2
        + [pltpu.SemaphoreType.DMA((slots,))] * 4
        + [pltpu.SemaphoreType.DMA((2 * head_count - 2,))] * 2,
        compiler_params=pltpu.CompilerParams(collective_id=0, has_side_effects=True),
    )(
        queries,
        cell_types[None],
        promoters[None],
        offsets[None],
        cell_embed,
        bin_keys,
        bin_values,
        w_out,
        slopes,
    )
    return result.astype(jnp.bfloat16)


def solution(mesh):
    return jax.shard_map(
        local,
        mesh=mesh,
        in_specs=(
            P("seq", "head"),
            P("seq"),
            P("seq"),
            P("seq"),
            P(None, "head"),
            P("seq", "head"),
            P("seq", "head"),
            P("head"),
            P("head", None),
        ),
        out_specs=P("seq", "head"),
        check_vma=False,
    )
```
